32 devices in a mesh: row: 8 (over z, x), col: 4 (over y, core).
Axes of the slice: x: 2, y: 2, z: 4, core: 2. Of those that a mesh axis runs over, the one named last changes fastest.
Arguments:
- diagonal: float32 [32, 512, 512], P(('row', 'col')), may hold values from -0.05 to 1.05
- lower: float32 [32, 512, 512], P(('row', 'col')), may hold values from -1 to 1, as said below
- upper: float32 [32, 512, 512], P(('row', 'col')), may hold values from -1 to 1, as said below
- right_side: float32 [32, 512, 128], P(('row', 'col')), may hold values from -6 to 6
- guess: float32 [32, 512, 128], P(('row', 'col')), may hold values from -4 to 4
Outputs:
- solution: float32 [32, 512, 128], P(('row', 'col'))
The draws below stay inside these ranges and needn't reach their ends.
Inputs may be any that keep to these rules, and one draw needn't show every extreme that they name: `lower`: each block is one half of an orthogonal matrix. `upper`: each block is one half of an orthogonal matrix.
All inputs are finite; a program needn't handle non-finite values.
Results may differ from the reference program's by a relative error of at most 0.00026.
Values sent between devices are 32-bit elements; how exact they have to be, the bound alone decides.
A program may use at most 64 MiB of HBM per device.

```python
import jax
import jax.numpy as jnp
from jax import lax

B = 512
R = 128
LEVELS = 2
NEWTON = 2
NB = 32


def draw_diagonal(key, part):
    scale = 0.025 / B ** 0.5
    shift_key = jax.random.fold_in(key, 5)
    noise_key = jax.random.fold_in(key, 7)
    shift = jax.random.uniform(shift_key, (NB,), jnp.float32, 1.004, 1.009)
    noise = jnp.clip(jax.random.normal(noise_key, (NB, B, B), jnp.float32), -6.0, 6.0) * scale
    return shift[:, None, None] * jnp.eye(B, dtype=jnp.float32) + noise


def half_orthogonal(key):
    gauss = jax.random.normal(key, (NB, B, B), jnp.float32)
    basis, upper_tri = jnp.linalg.qr(gauss)
    signs = jnp.sign(jnp.diagonal(upper_tri, axis1=1, axis2=2)) + (jnp.diagonal(upper_tri, axis1=1, axis2=2) == 0)
    return 0.5 * basis * signs[:, None, :]


def coupling_basis(key):
    return half_orthogonal(jax.random.fold_in(key, 11))


def draw_lower(key, part):
    return -coupling_basis(key)


def draw_upper(key, part):
    following = jnp.roll(coupling_basis(key), -1, axis=0)
    return -jnp.swapaxes(following, 1, 2)


def level_of(key, shape, shards, smallest, largest):
    def one(dim, blocks):
        heights = jax.random.uniform(jax.random.fold_in(jax.random.fold_in(key, 6), dim), (blocks,), jnp.float32, smallest / len(shards), largest / len(shards))
        return jnp.repeat(jnp.exp(heights), shape[dim] // blocks).reshape((-1,) + (1,) * (len(shape) - dim - 1))

    factor_of = one(*shards[0])
    for cut in shards[1:]:
        factor_of = factor_of * one(*cut)
    return factor_of


def scatter_about(stream_key, extent, deviation, most, cuts=(), held_as=jnp.bfloat16):
    drawn = jax.random.normal(stream_key, extent, jnp.float32) * deviation
    if len(cuts) > 0:
        drawn = level_of(stream_key, extent, cuts, -0.22, 0.18) * drawn
    return jnp.clip(drawn, min=-most, max=most).astype(held_as)


def setup_inputs(seed: int = 0) -> dict:
    streams_of = jax.random.split(jax.random.key(seed), 6)
    return {
        "diagonal": draw_diagonal(jax.random.fold_in(streams_of[5], 71), 0),
        "lower": draw_lower(jax.random.fold_in(streams_of[5], 71), 0),
        "upper": draw_upper(jax.random.fold_in(streams_of[5], 71), 0),
        "right_side": scatter_about(streams_of[3], (NB, B, R), 1.0, 6.0, ((0, 32),), jnp.float32),
        "guess": scatter_about(streams_of[4], (NB, B, R), 1.0, 4.0, ((0, 32),), jnp.float32),
    }


def multiply(left, right):
    return jnp.matmul(left, right, precision=lax.Precision.HIGHEST)

def invert(matrix):
    order = matrix.shape[-1]
    eye = jnp.eye(order, dtype=jnp.float32)
    mean_diag = jnp.trace(matrix, axis1=-2, axis2=-1) / order
    approx = eye / mean_diag[..., None, None]
    for step in range(NEWTON):
        approx = multiply(approx, 2.0 * eye - multiply(matrix, approx))
    return approx

def from_before(array, stride):
    return jnp.concatenate([jnp.zeros_like(array[:stride]), array[:-stride]], axis=0)

def from_after(array, stride):
    return jnp.concatenate([array[stride:], jnp.zeros_like(array[:stride])], axis=0)

def reference(diagonal, lower, upper, right_side, guess):
    count = diagonal.shape[0]
    rows = jnp.arange(count, dtype=jnp.int32)[:, None, None]
    low = jnp.where(rows == 0, jnp.float32(0.0), lower)
    up = jnp.where(rows == count - 1, jnp.float32(0.0), upper)
    diag = diagonal
    rhs = right_side
    for level in range(LEVELS):
        stride = 2 ** level
        pivot = invert(diag)
        scaled_low = multiply(pivot, low)
        scaled_up = multiply(pivot, up)
        scaled_rhs = multiply(pivot, rhs)
        new_diag = diag - multiply(low, from_before(scaled_up, stride)) - multiply(up, from_after(scaled_low, stride))
        new_rhs = rhs - multiply(low, from_before(scaled_rhs, stride)) - multiply(up, from_after(scaled_rhs, stride))
        new_low = -multiply(low, from_before(scaled_low, stride))
        new_up = -multiply(up, from_after(scaled_up, stride))
        diag, low, up, rhs = (new_diag, new_low, new_up, new_rhs)
    reach = 2 ** LEVELS
    inner = rhs - multiply(low, from_before(guess, reach)) - multiply(up, from_after(guess, reach))
    return multiply(invert(diag), inner)
```

```python
import functools
from collections import namedtuple

import jax
import jax.numpy as jnp
from jax import lax
from jax.experimental import pallas as pl
from jax.experimental.pallas import tpu as pltpu
from jax.sharding import PartitionSpec as P

AXES = ("row", "col")
F32, BF16 = jnp.float32, jnp.bfloat16
CHUNKS = 2

MESSAGES = (
    ("a1", "partner", CHUNKS), ("a2", "partner", CHUNKS), ("b", "partner", 0), ("gp", "partner", 0),
    ("q", "partner", CHUNKS), ("wp", "partner", 0),
    ("lx", "side", 1), ("s1", "side", CHUNKS), ("st", "side", 0), ("gi", "side", 0), ("lp", "side", CHUNKS),
    ("sol", "side", 0),
    ("n", "tip", CHUNKS),
    ("k", "far", CHUNKS), ("z", "far", 0), ("sz", "far", 0),
)
FIRST, PEER = {}, {}
TOTAL = 0
for _name, _peer, _count in MESSAGES:
    FIRST[_name], PEER[_name] = TOTAL, _peer
    TOTAL += max(_count, 1)


def scratch_types(order, columns):
    matrix = pltpu.VMEM((order, order), F32)
    chunked = pltpu.VMEM((CHUNKS, order, order // CHUNKS), F32)
    vector = pltpu.VMEM((order, columns), F32)
    pair = pltpu.VMEM((2, order, order), BF16)
    types = dict(diag=matrix, c1=matrix, c2=matrix, rhs=vector, g=vector)
    types.update({name: chunked for name in ("sa1", "sa2", "sq", "sk", "sd")})
    types.update({name: vector for name in ("sb", "st", "swp", "sz", "ssz", "ssol", "pr", "acc")})
    for name, _, count in MESSAGES:
        types["r_" + name] = vector if count == 0 else matrix if count == 1 else chunked
    types.update({name: pair for name in ("d2", "x2", "y2", "p2", "in2", "k2", "t2", "u2", "pq2")})
    types.update(coup=pltpu.VMEM((4, 2, order, order), BF16), prod=pltpu.VMEM((5, 2, order, order), BF16))
    types.update(vec2=pltpu.VMEM((2, order, columns), BF16))
    types.update(load_sem=pltpu.SemaphoreType.DMA((5,)))
    types.update(send_sem=pltpu.SemaphoreType.DMA((TOTAL,)), recv_sem=pltpu.SemaphoreType.DMA((TOTAL,)))
    return types


def kernel(chain, across, names, d_hbm, low_hbm, up_hbm, b_hbm, g_hbm, out_ref, *scratch):
    s = namedtuple("Scratch", names)(*scratch)
    order = s.diag.shape[0]
    width = order // CHUNKS
    place = lax.axis_index("row") * across + lax.axis_index("col")
    role = lax.rem(place, 4)
    outer = (role == 0) | (role == 3)
    inner = (role == 1) | (role == 2)
    left = role < 2
    right = role >= 2
    away = 2 * lax.rem(place, 2) - 1
    has_side = (place + away >= 0) & (place + away < chain)
    has_far = (place + 3 * away >= 0) & (place + 3 * away < chain)

    def device(offset):
        index = lax.rem(place + offset + chain, chain)
        return (index // across, lax.rem(index, across))

    peers = {
        "partner": device(-away), "side": device(away), "far": device(3 * away),
        "tip": device(jnp.where(left, 2, -2)),
    }
    sent_if = {name: {"partner": None, "side": has_side, "far": has_far, "tip": outer}[peer] for name, peer in PEER.items()}
    came_if = {name: {"partner": None, "side": has_side, "far": has_far, "tip": inner}[peer] for name, peer in PEER.items()}
    for name in ("lx", "gi", "lp", "sol"):
        sent_if[name] = came_if[name] = inner

    def guarded(condition, action):
        if condition is None:
            action()
        else:
            pl.when(condition)(action)

    def copy(name, src, chunk):
        dst = getattr(s, "r_" + name)
        index = FIRST[name] + chunk
        if dst.ndim == 3:
            dst = dst.at[chunk]
        return pltpu.make_async_remote_copy(
            src_ref=src if src is not None else dst,
            dst_ref=dst,
            send_sem=s.send_sem.at[index],
            recv_sem=s.recv_sem.at[index],
            device_id=peers[PEER[name]],
            device_id_type=pl.DeviceIdType.MESH,
        )

    def send(name, src, chunk=0, also=None):
        condition = sent_if[name]
        if also is not None:
            condition = also if condition is None else condition & also
        guarded(condition, lambda: copy(name, src, chunk).start())

    def receive(name, chunk=0):
        guarded(came_if[name], lambda: copy(name, None, chunk).wait_recv())

    sent = []

    def settle(name, chunk=0):
        sent.append((name, chunk))
        guarded(sent_if[name], lambda: copy(name, None, chunk).wait_send())

    def load(src, dst, index):
        return pltpu.make_async_copy(src.at[0], dst, s.load_sem.at[index])

    def load_c1(act):
        pl.when(has_side & left)(lambda: act(load(low_hbm, s.c1, 1)))
        pl.when(has_side & right)(lambda: act(load(up_hbm, s.c1, 1)))

    def load_c2(act):
        pl.when(left)(lambda: act(load(up_hbm, s.c2, 2)))
        pl.when(right)(lambda: act(load(low_hbm, s.c2, 2)))

    load(d_hbm, s.diag, 0).start()
    load_c2(lambda c: c.start())
    load_c1(lambda c: c.start())
    load(b_hbm, s.rhs, 3).start()
    load(g_hbm, s.g, 4).start()

    barrier = pltpu.get_barrier_semaphore()
    for side, condition in (("partner", None), ("tip", None), ("side", has_side), ("far", has_far)):
        guarded(condition, lambda: pl.semaphore_signal(
            barrier, inc=1, device_id=peers[side], device_id_type=pl.DeviceIdType.MESH))
    pl.semaphore_wait(barrier, 2 + jnp.where(has_side, 1, 0) + jnp.where(has_far, 1, 0))

    load_c2(lambda c: c.wait())
    send("lx", s.c2)
    send("gp", g_hbm.at[0], also=outer)

    def zero(*refs):
        for ref in refs:
            ref[...] = jnp.zeros_like(ref)

    pl.when(jnp.logical_not(has_side))(lambda: zero(s.c1, s.r_s1, s.r_st))
    pl.when(jnp.logical_not(has_far))(lambda: zero(s.r_k, s.r_z, s.r_sz))

    def cols(chunk):
        return slice(chunk * width, (chunk + 1) * width)

    def put(pair, value, where=slice(None)):
        high = value.astype(BF16)
        pair[0, :, where] = high
        pair[1, :, where] = (value - high.astype(F32)).astype(BF16)

    def dot(left, right):
        return jnp.dot(left, right, preferred_element_type=F32)

    def multiply(left, right, where=slice(None), inside=slice(None)):
        first, second = left[0, :, inside], left[1, :, inside]
        high, low = right[0, inside, where], right[1, inside, where]
        return dot(first, high) + (dot(first, low) + dot(second, high))

    def eye(chunk):
        rows = lax.broadcasted_iota(jnp.int32, (order, width), 0)
        return (rows == lax.broadcasted_iota(jnp.int32, (order, width), 1) + chunk * width).astype(F32)

    def mean_diag():
        total = jnp.float32(0.0)
        for c in range(CHUNKS):
            total += jnp.sum(eye(c) * s.diag[:, cols(c)])
        return total / order

    def invert():
        scale = 1.0 / mean_diag()
        for c in range(CHUNKS):
            block = s.diag[:, cols(c)]
            put(s.d2, block, cols(c))
            put(s.x2, (2.0 * eye(c) - block * scale) * scale, cols(c))
        for c in range(CHUNKS):
            put(s.y2, 2.0 * eye(c) - multiply(s.d2, s.x2, cols(c)), cols(c))
        for c in range(CHUNKS):
            put(s.p2, multiply(s.x2, s.y2, cols(c)), cols(c))

    def times(left, vector):
        put(s.vec2, vector)
        return multiply(left, s.vec2)

    def coup(index):
        return s.coup.at[index]

    def prod(index):
        return s.prod.at[index]

    beyond = prod(4)
    outward = coup(jnp.where(outer, 0, 3))
    inward = coup(jnp.where(outer, 1, 2))

    load(d_hbm, s.diag, 0).wait()
    invert()
    load_c1(lambda c: c.wait())
    put(coup(0), s.c1[...])
    for c in range(CHUNKS):
        block = multiply(s.p2, coup(0), cols(c))
        s.sa1[c] = block
        send("s1", s.sa1.at[c], c, also=outer)
        send("a1", s.sa1.at[c], c)
        put(prod(0), block, cols(c))
    put(coup(1), s.c2[...])
    for c in range(CHUNKS):
        block = multiply(s.p2, coup(1), cols(c))
        s.sa2[c] = block
        send("a2", s.sa2.at[c], c)
        put(prod(1), block, cols(c))
    for c in range(CHUNKS):
        receive("a2", c)
        put(prod(3), s.r_a2[c], cols(c))

        @pl.when(inner)
        def _():
            s.sd[c] = s.diag[:, cols(c)] - multiply(coup(0), prod(3), cols(c))

        send("s1", s.sd.at[c], c, also=inner)
    load(b_hbm, s.rhs, 3).wait()
    s.sb[...] = times(s.p2, s.rhs[...])
    send("b", s.sb)
    receive("b")

    @pl.when(inner)
    def _():
        s.st[...] = s.rhs[...] - times(coup(0), s.r_b[...])

    receive("lx")

    @pl.when(inner)
    def _():
        put(coup(2), s.r_lx[...])

    second = prod(jnp.where(outer, 3, 0))
    for c in range(CHUNKS):
        put(s.in2, -multiply(inward, second, cols(c)), cols(c))
    for c in range(CHUNKS):
        receive("a1", c)
        put(prod(2), s.r_a1[c], cols(c))
    load(g_hbm, s.g, 4).wait()
    for c in range(CHUNKS):
        settle("s1", c)
    for c in range(CHUNKS):
        send("n", s.sa2.at[c], c)
    send("st", s.sb, also=outer)
    send("st", s.st, also=inner)
    send("gi", g_hbm.at[0])
    for c in range(CHUNKS):
        send("lp", s.c1.at[:, cols(c)], c)

    first = prod(jnp.where(outer, 2, 1))
    for c in range(CHUNKS):
        receive("s1", c)

        @pl.when(outer)
        def _():
            put(beyond, s.r_s1[c], cols(c))
            s.diag[:, cols(c)] = s.diag[:, cols(c)] - multiply(coup(0), beyond, cols(c))

        @pl.when(inner)
        def _():
            s.diag[:, cols(c)] = s.r_s1[c]

        s.diag[:, cols(c)] = s.diag[:, cols(c)] - multiply(inward, first, cols(c))

    invert()

    def scaled():
        for c in range(CHUNKS):
            put(s.k2, multiply(beyond, s.p2, cols(c)), cols(c))

    def far_chunk(c):
        s.sk[c] = multiply(s.k2, outward, cols(c))
        send("k", s.sk.at[c], c)

    @pl.when(outer)
    def _():
        s.ssz[...] = times(beyond, s.g[...])
        send("sz", s.ssz)
        scaled()
        for c in range(CHUNKS):
            far_chunk(c)

    for c in range(CHUNKS):
        s.sq[c] = multiply(s.p2, s.in2, cols(c))
        send("q", s.sq.at[c], c)

    receive("gi")

    @pl.when(inner)
    def _():
        s.g[...] = s.r_gi[...]

    send("gp", s.r_gi, also=inner)
    receive("st")

    @pl.when(outer)
    def _():
        s.rhs[...] = s.rhs[...] - times(coup(0), s.r_st[...]) - times(inward, s.r_b[...])

    @pl.when(inner)
    def _():
        s.rhs[...] = s.r_st[...] - times(inward, s.sb[...])

    receive("gp")
    s.pr[...] = times(s.p2, s.rhs[...] - times(s.in2, s.r_gp[...]))
    for c in range(CHUNKS):
        receive("n", c)

        @pl.when(inner)
        def _():
            put(beyond, s.r_n[c], cols(c))

    s.sz[...] = times(beyond, s.pr[...])
    send("z", s.sz)

    @pl.when(inner)
    def _():
        s.ssz[...] = times(beyond, s.g[...])
        send("sz", s.ssz)
        scaled()

    for c in range(CHUNKS):
        receive("lp", c)

        @pl.when(inner)
        def _():
            put(coup(3), s.r_lp[c], cols(c))
            far_chunk(c)

    for c in range(CHUNKS):
        receive("q", c)
        put(s.pq2, s.r_q[c], cols(c))
        s.diag[:, cols(c)] = s.diag[:, cols(c)] - multiply(s.in2, s.pq2, cols(c))
    receive("sz")
    s.swp[...] = times(s.p2, s.rhs[...] + times(outward, s.r_sz[...]))
    send("wp", s.swp)
    receive("z")
    s.acc[...] = s.rhs[...] + times(outward, s.r_z[...])
    receive("wp")
    s.acc[...] = s.acc[...] - times(s.in2, s.r_wp[...])

    for c in range(CHUNKS):
        receive("k", c)
        put(s.t2, s.r_k[c], cols(c))
        put(s.u2, multiply(outward, s.t2, cols(c)), cols(c))
        for e in range(CHUNKS):
            s.diag[:, cols(e)] = s.diag[:, cols(e)] - multiply(s.u2, beyond, cols(e), cols(c))

    put(s.d2, s.diag[...])
    scale = 1.0 / mean_diag()
    value = s.acc[...]
    half = (2.0 * value - times(s.d2, value) * scale) * scale
    rest = 2.0 * value - times(s.d2, half)
    result = (2.0 * rest - times(s.d2, rest) * scale) * scale

    @pl.when(outer)
    def _():
        out_ref[...] = result

    @pl.when(inner)
    def _():
        s.ssol[...] = result
        send("sol", s.ssol)
        receive("sol")
        out_ref[...] = s.r_sol[...]

    for name, _, count in MESSAGES:
        for chunk in range(max(count, 1)):
            if (name, chunk) not in sent:
                settle(name, chunk)


def body(diagonal, lower, upper, right_side, guess):
    across = lax.axis_size("col")
    chain = lax.axis_size("row") * across
    order, columns = right_side.shape[1:]
    types = scratch_types(order, columns)
    result = pl.pallas_call(
        functools.partial(kernel, chain, across, tuple(types)),
        out_shape=jax.ShapeDtypeStruct((order, columns), F32),
        in_specs=[pl.BlockSpec(memory_space=pl.ANY)] * 5,
        out_specs=pl.BlockSpec(memory_space=pltpu.VMEM),
        scratch_shapes=list(types.values()),
        compiler_params=pltpu.CompilerParams(
            collective_id=0, has_side_effects=True, vmem_limit_bytes=52 * 2**20),
    )(diagonal, lower, upper, right_side, guess)
    return result[None]


def solution(mesh):
    spec = P(AXES, None, None)
    return jax.shard_map(body, mesh=mesh, in_specs=(spec,) * 5, out_specs=spec, check_vma=False)
```

```python
import functools
from collections import namedtuple

import jax
import jax.numpy as jnp
from jax import lax
from jax.experimental import pallas as pl
from jax.experimental.pallas import tpu as pltpu
from jax.sharding import PartitionSpec as P

AXES = ("row", "col")
F32, BF16 = jnp.float32, jnp.bfloat16
CHUNKS = 2
FINE = 4

MESSAGES = (
    ("a1", "partner", CHUNKS), ("a2", "partner", CHUNKS), ("b", "partner", 0), ("gp", "partner", 0),
    ("q", "partner", CHUNKS), ("wp", "partner", 0),
    ("lx", "side", 1), ("s1", "side", CHUNKS), ("st", "side", 0), ("gi", "side", 0), ("lp", "side", FINE), ("n", "side", CHUNKS),
    ("sol", "side", 0),
    ("k", "far", FINE), ("z", "far", 0), ("sz", "far", 0),
)
FIRST, PEER = {}, {}
TOTAL = 0
for _name, _peer, _count in MESSAGES:
    FIRST[_name], PEER[_name] = TOTAL, _peer
    TOTAL += max(_count, 1)


def scratch_types(order, columns):
    matrix = pltpu.VMEM((order, order), F32)
    chunked = pltpu.VMEM((CHUNKS, order, order // CHUNKS), F32)
    vector = pltpu.VMEM((order, columns), F32)
    pair = pltpu.VMEM((2, order, order), BF16)
    types = dict(diag=matrix, c1=matrix, c2=matrix, rhs=vector, g=vector)
    fine = pltpu.VMEM((FINE, order, order // FINE), F32)
    types.update({name: chunked for name in ("sa1", "sa2", "sq", "sd")})
    types.update(sk=fine)
    types.update({name: vector for name in ("sb", "st", "swp", "sz", "ssz", "ssol", "pr", "acc")})
    for name, _, count in MESSAGES:
        types["r_" + name] = {0: vector, 1: matrix, CHUNKS: chunked, FINE: fine}[count]
    types.update({name: pair for name in ("d2", "x2", "y2", "p2", "in2", "k2", "t2", "u2", "pq2")})
    types.update(coup=pltpu.VMEM((4, 2, order, order), BF16), prod=pltpu.VMEM((5, 2, order, order), BF16))
    types.update(vec2=pltpu.VMEM((2, order, columns), BF16))
    types.update(load_sem=pltpu.SemaphoreType.DMA((5,)))
    types.update(send_sem=pltpu.SemaphoreType.DMA((TOTAL,)), recv_sem=pltpu.SemaphoreType.DMA((TOTAL,)))
    return types


def kernel(chain, across, names, d_hbm, low_hbm, up_hbm, b_hbm, g_hbm, out_ref, *scratch):
    s = namedtuple("Scratch", names)(*scratch)
    order = s.diag.shape[0]
    width = order // CHUNKS
    place = lax.axis_index("row") * across + lax.axis_index("col")
    role = lax.rem(place, 4)
    outer = (role == 0) | (role == 3)
    inner = (role == 1) | (role == 2)
    left = role < 2
    right = role >= 2
    away = 2 * lax.rem(place, 2) - 1
    has_side = (place + away >= 0) & (place + away < chain)
    has_far = (place + 3 * away >= 0) & (place + 3 * away < chain)

    def device(offset):
        index = lax.rem(place + offset + chain, chain)
        return (index // across, lax.rem(index, across))

    peers = {"partner": device(-away), "side": device(away), "far": device(3 * away)}
    exists = {"partner": None, "side": has_side, "far": has_far}
    only_if = {name: exists[peer] for name, peer in PEER.items()}
    only_if.update({name: inner for name in ("lx", "gi", "n", "lp", "sol")})

    def guarded(condition, action):
        if condition is None:
            action()
        else:
            pl.when(condition)(action)

    def copy(name, src, chunk):
        dst = getattr(s, "r_" + name)
        index = FIRST[name] + chunk
        if dst.ndim == 3:
            dst = dst.at[chunk]
        return pltpu.make_async_remote_copy(
            src_ref=src if src is not None else dst,
            dst_ref=dst,
            send_sem=s.send_sem.at[index],
            recv_sem=s.recv_sem.at[index],
            device_id=peers[PEER[name]],
            device_id_type=pl.DeviceIdType.MESH,
        )

    def send(name, src, chunk=0, also=None):
        condition = only_if[name]
        if also is not None:
            condition = also if condition is None else condition & also
        guarded(condition, lambda: copy(name, src, chunk).start())

    def receive(name, chunk=0):
        guarded(only_if[name], lambda: copy(name, None, chunk).wait_recv())

    def load(src, dst, index):
        return pltpu.make_async_copy(src.at[0], dst, s.load_sem.at[index])

    def load_c1(act):
        pl.when(has_side & left)(lambda: act(load(low_hbm, s.c1, 1)))
        pl.when(has_side & right)(lambda: act(load(up_hbm, s.c1, 1)))

    def load_c2(act):
        pl.when(left)(lambda: act(load(up_hbm, s.c2, 2)))
        pl.when(right)(lambda: act(load(low_hbm, s.c2, 2)))

    load(d_hbm, s.diag, 0).start()
    load_c2(lambda c: c.start())
    load_c1(lambda c: c.start())
    load(b_hbm, s.rhs, 3).start()
    load(g_hbm, s.g, 4).start()

    barrier = pltpu.get_barrier_semaphore()
    for side, condition in (("partner", None), ("side", has_side), ("far", has_far)):
        guarded(condition, lambda: pl.semaphore_signal(
            barrier, inc=1, device_id=peers[side], device_id_type=pl.DeviceIdType.MESH))
    pl.semaphore_wait(barrier, 1 + jnp.where(has_side, 1, 0) + jnp.where(has_far, 1, 0))

    load_c2(lambda c: c.wait())
    send("lx", s.c2)
    send("gp", g_hbm.at[0], also=outer)

    def zero(*refs):
        for ref in refs:
            ref[...] = jnp.zeros_like(ref)

    pl.when(jnp.logical_not(has_side))(lambda: zero(s.c1, s.r_s1, s.r_st))
    pl.when(jnp.logical_not(has_far))(lambda: zero(s.r_k, s.r_z, s.r_sz))

    def cols(chunk, pieces=CHUNKS):
        return slice(chunk * (order // pieces), (chunk + 1) * (order // pieces))

    def put(pair, value, where=slice(None)):
        high = value.astype(BF16)
        pair[0, :, where] = high
        pair[1, :, where] = (value - high.astype(F32)).astype(BF16)

    def dot(left, right):
        return jnp.dot(left, right, preferred_element_type=F32)

    def multiply(left, right, where=slice(None), inside=slice(None)):
        first, second = left[0, :, inside], left[1, :, inside]
        high, low = right[0, inside, where], right[1, inside, where]
        return dot(first, high) + (dot(first, low) + dot(second, high))

    def eye(chunk):
        rows = lax.broadcasted_iota(jnp.int32, (order, width), 0)
        return (rows == lax.broadcasted_iota(jnp.int32, (order, width), 1) + chunk * width).astype(F32)

    def mean_diag():
        total = jnp.float32(0.0)
        for c in range(CHUNKS):
            total += jnp.sum(eye(c) * s.diag[:, cols(c)])
        return total / order

    def invert():
        scale = 1.0 / mean_diag()
        for c in range(CHUNKS):
            block = s.diag[:, cols(c)]
            put(s.d2, block, cols(c))
            put(s.x2, (2.0 * eye(c) - block * scale) * scale, cols(c))
        for c in range(CHUNKS):
            put(s.y2, 2.0 * eye(c) - multiply(s.d2, s.x2, cols(c)), cols(c))
        for c in range(CHUNKS):
            put(s.p2, multiply(s.x2, s.y2, cols(c)), cols(c))

    def times(left, vector):
        put(s.vec2, vector)
        return multiply(left, s.vec2)

    def coup(index):
        return s.coup.at[index]

    def prod(index):
        return s.prod.at[index]

    beyond = prod(4)
    outward = coup(jnp.where(outer, 0, 3))
    inward = coup(jnp.where(outer, 1, 2))

    load(d_hbm, s.diag, 0).wait()
    invert()
    load_c1(lambda c: c.wait())
    put(coup(0), s.c1[...])
    for c in range(CHUNKS):
        block = multiply(s.p2, coup(0), cols(c))
        s.sa1[c] = block
        send("s1", s.sa1.at[c], c, also=outer)
        send("a1", s.sa1.at[c], c)
        put(prod(0), block, cols(c))
    put(coup(1), s.c2[...])
    for c in range(CHUNKS):
        block = multiply(s.p2, coup(1), cols(c))
        s.sa2[c] = block
        send("a2", s.sa2.at[c], c)
        put(prod(1), block, cols(c))
    for c in range(CHUNKS):
        receive("a2", c)
        put(prod(3), s.r_a2[c], cols(c))

        @pl.when(inner)
        def _():
            s.sd[c] = s.diag[:, cols(c)] - multiply(coup(0), prod(3), cols(c))

        send("s1", s.sd.at[c], c, also=inner)
    load(b_hbm, s.rhs, 3).wait()
    s.sb[...] = times(s.p2, s.rhs[...])
    send("b", s.sb)
    receive("b")

    @pl.when(inner)
    def _():
        s.st[...] = s.rhs[...] - times(coup(0), s.r_b[...])

    send("gi", g_hbm.at[0])
    for c in range(CHUNKS):
        send("n", s.r_a2.at[c], c)
    send("st", s.st, also=inner)
    for c in range(FINE):
        send("lp", s.c1.at[:, cols(c, FINE)], c)

    receive("lx")

    @pl.when(inner)
    def _():
        put(coup(2), s.r_lx[...])

    second = prod(jnp.where(outer, 3, 0))
    for c in range(CHUNKS):
        put(s.in2, -multiply(inward, second, cols(c)), cols(c))
    for c in range(CHUNKS):
        receive("a1", c)
        put(prod(2), s.r_a1[c], cols(c))
    load(g_hbm, s.g, 4).wait()

    first = prod(jnp.where(outer, 2, 1))
    for c in range(CHUNKS):
        receive("s1", c)

        @pl.when(outer)
        def _():
            put(beyond, s.r_s1[c], cols(c))
            s.diag[:, cols(c)] = s.diag[:, cols(c)] - multiply(coup(0), beyond, cols(c))

        @pl.when(inner)
        def _():
            s.diag[:, cols(c)] = s.r_s1[c]

        s.diag[:, cols(c)] = s.diag[:, cols(c)] - multiply(inward, first, cols(c))

    invert()

    def scaled():
        for c in range(CHUNKS):
            put(s.k2, multiply(beyond, s.p2, cols(c)), cols(c))
        s.ssz[...] = times(beyond, s.g[...])
        send("sz", s.ssz)

    def far_piece(c):
        s.sk[c] = multiply(s.k2, outward, cols(c, FINE))
        send("k", s.sk.at[c], c)

    @pl.when(outer)
    def _():
        scaled()
        for c in range(FINE):
            far_piece(c)

    for c in range(CHUNKS):
        s.sq[c] = multiply(s.p2, s.in2, cols(c))
        send("q", s.sq.at[c], c)

    receive("gi")

    @pl.when(inner)
    def _():
        s.g[...] = s.r_gi[...]

    send("gp", s.r_gi, also=inner)
    receive("gp")
    send("st", s.sb, also=outer)
    for c in range(CHUNKS):
        receive("q", c)
        put(s.pq2, s.r_q[c], cols(c))
        s.diag[:, cols(c)] = s.diag[:, cols(c)] - multiply(s.in2, s.pq2, cols(c))
    for c in range(CHUNKS):
        receive("n", c)

        @pl.when(inner)
        def _():
            put(beyond, s.r_n[c], cols(c))

    @pl.when(inner)
    def _():
        scaled()

    receive("st")

    @pl.when(outer)
    def _():
        s.rhs[...] = s.rhs[...] - times(coup(0), s.r_st[...]) - times(inward, s.r_b[...])

    @pl.when(inner)
    def _():
        s.rhs[...] = s.r_st[...] - times(inward, s.sb[...])

    s.pr[...] = times(s.p2, s.rhs[...] - times(s.in2, s.r_gp[...]))
    s.sz[...] = times(beyond, s.pr[...])
    send("z", s.sz)

    @pl.when(inner)
    def _():
        for c in range(FINE):
            receive("k", c)
            put(s.t2, s.r_k[c], cols(c, FINE))
        for c in range(CHUNKS):
            put(s.u2, multiply(s.t2, beyond, cols(c)), cols(c))
        for c in range(FINE):
            receive("lp", c)
            put(coup(3), s.r_lp[c], cols(c, FINE))
            far_piece(c)
            for e in range(CHUNKS):
                s.diag[:, cols(e)] = s.diag[:, cols(e)] - multiply(coup(3), s.u2, cols(e), cols(c, FINE))

    receive("sz")
    s.swp[...] = times(s.p2, s.rhs[...] + times(outward, s.r_sz[...]))
    send("wp", s.swp)
    receive("z")
    s.acc[...] = s.rhs[...] + times(outward, s.r_z[...])
    receive("wp")
    s.acc[...] = s.acc[...] - times(s.in2, s.r_wp[...])

    @pl.when(outer)
    def _():
        for c in range(FINE):
            receive("k", c)
            put(s.t2, s.r_k[c], cols(c, FINE))
            put(s.u2, multiply(outward, s.t2, cols(c, FINE)), cols(c, FINE))
            for e in range(CHUNKS):
                s.diag[:, cols(e)] = s.diag[:, cols(e)] - multiply(s.u2, beyond, cols(e), cols(c, FINE))

    put(s.d2, s.diag[...])
    scale = 1.0 / mean_diag()
    value = s.acc[...]
    half = (2.0 * value - times(s.d2, value) * scale) * scale
    rest = 2.0 * value - times(s.d2, half)
    result = (2.0 * rest - times(s.d2, rest) * scale) * scale

    @pl.when(outer)
    def _():
        out_ref[...] = result

    @pl.when(inner)
    def _():
        s.ssol[...] = result
        send("sol", s.ssol)
        receive("sol")
        out_ref[...] = s.r_sol[...]

    for name, _, count in MESSAGES:
        for chunk in range(max(count, 1)):
            guarded(only_if[name], lambda: copy(name, None, chunk).wait_send())


def body(diagonal, lower, upper, right_side, guess):
    across = lax.axis_size("col")
    chain = lax.axis_size("row") * across
    order, columns = right_side.shape[1:]
    types = scratch_types(order, columns)
    result = pl.pallas_call(
        functools.partial(kernel, chain, across, tuple(types)),
        out_shape=jax.ShapeDtypeStruct((order, columns), F32),
        in_specs=[pl.BlockSpec(memory_space=pl.ANY)] * 5,
        out_specs=pl.BlockSpec(memory_space=pltpu.VMEM),
        scratch_shapes=list(types.values()),
        compiler_params=pltpu.CompilerParams(
            collective_id=0, has_side_effects=True, vmem_limit_bytes=52 * 2**20),
    )(diagonal, lower, upper, right_side, guess)
    return result[None]


def solution(mesh):
    spec = P(AXES, None, None)
    return jax.shard_map(body, mesh=mesh, in_specs=(spec,) * 5, out_specs=spec, check_vma=False)
```

```python
import functools
from collections import namedtuple

import jax
import jax.numpy as jnp
from jax import lax
from jax.experimental import pallas as pl
from jax.experimental.pallas import tpu as pltpu
from jax.sharding import PartitionSpec as P

AXES = ("row", "col")
F32, BF16 = jnp.float32, jnp.bfloat16
CHUNKS = 2
FINE = 4

MESSAGES = (
    ("a1", "partner", CHUNKS), ("a2", "partner", CHUNKS), ("b", "partner", 0), ("gp", "partner", 0),
    ("q", "partner", CHUNKS), ("wp", "partner", 0),
    ("lx", "side", 1), ("s1", "side", CHUNKS), ("st", "side", 0), ("gi", "side", 0), ("lp", "side", FINE), ("n", "side", CHUNKS),
    ("sol", "side", 0),
    ("k", "far", FINE), ("z", "far", 0), ("sz", "far", 0),
)
FIRST, PEER = {}, {}
TOTAL = 0
for _name, _peer, _count in MESSAGES:
    FIRST[_name], PEER[_name] = TOTAL, _peer
    TOTAL += max(_count, 1)


def scratch_types(order, columns):
    matrix = pltpu.VMEM((order, order), F32)
    chunked = pltpu.VMEM((CHUNKS, order, order // CHUNKS), F32)
    vector = pltpu.VMEM((order, columns), F32)
    pair = pltpu.VMEM((2, order, order), BF16)
    types = dict(diag=matrix, c1=matrix, c2=matrix, rhs=vector, g=vector)
    fine = pltpu.VMEM((FINE, order, order // FINE), F32)
    types.update({name: chunked for name in ("sa1", "sa2", "sq", "sd")})
    types.update(sk=fine)
    types.update({name: vector for name in ("sb", "st", "swp", "sz", "ssz", "ssol", "pr", "acc")})
    for name, _, count in MESSAGES:
        types["r_" + name] = {0: vector, 1: matrix, CHUNKS: chunked, FINE: fine}[count]
    types.update({name: pair for name in ("d2", "x2", "y2", "p2", "in2", "k2", "t2", "u2", "pq2")})
    types.update(coup=pltpu.VMEM((4, 2, order, order), BF16), prod=pltpu.VMEM((5, 2, order, order), BF16))
    types.update(vec2=pltpu.VMEM((2, order, columns), BF16))
    types.update(load_sem=pltpu.SemaphoreType.DMA((5,)))
    types.update(send_sem=pltpu.SemaphoreType.DMA((TOTAL,)), recv_sem=pltpu.SemaphoreType.DMA((TOTAL,)))
    return types


def kernel(chain, across, names, d_hbm, low_hbm, up_hbm, b_hbm, g_hbm, out_ref, *scratch):
    s = namedtuple("Scratch", names)(*scratch)
    order = s.diag.shape[0]
    width = order // CHUNKS
    place = lax.axis_index("row") * across + lax.axis_index("col")
    role = lax.rem(place, 4)
    outer = (role == 0) | (role == 3)
    inner = (role == 1) | (role == 2)
    left = role < 2
    right = role >= 2
    away = 2 * lax.rem(place, 2) - 1
    has_side = (place + away >= 0) & (place + away < chain)
    has_far = (place + 3 * away >= 0) & (place + 3 * away < chain)

    def device(offset):
        index = lax.rem(place + offset + chain, chain)
        return (index // across, lax.rem(index, across))

    peers = {"partner": device(-away), "side": device(away), "far": device(3 * away)}
    exists = {"partner": None, "side": has_side, "far": has_far}
    only_if = {name: exists[peer] for name, peer in PEER.items()}
    only_if.update({name: inner for name in ("lx", "gi", "n", "lp", "sol")})

    def guarded(condition, action):
        if condition is None:
            action()
        else:
            pl.when(condition)(action)

    def copy(name, src, chunk):
        dst = getattr(s, "r_" + name)
        index = FIRST[name] + chunk
        if dst.ndim == 3:
            dst = dst.at[chunk]
        return pltpu.make_async_remote_copy(
            src_ref=src if src is not None else dst,
            dst_ref=dst,
            send_sem=s.send_sem.at[index],
            recv_sem=s.recv_sem.at[index],
            device_id=peers[PEER[name]],
            device_id_type=pl.DeviceIdType.MESH,
        )

    def send(name, src, chunk=0, also=None):
        condition = only_if[name]
        if also is not None:
            condition = also if condition is None else condition & also
        guarded(condition, lambda: copy(name, src, chunk).start())

    def receive(name, chunk=0):
        guarded(only_if[name], lambda: copy(name, None, chunk).wait_recv())

    def load(src, dst, index):
        return pltpu.make_async_copy(src.at[0], dst, s.load_sem.at[index])

    def load_c1(act):
        pl.when(has_side & left)(lambda: act(load(low_hbm, s.c1, 1)))
        pl.when(has_side & right)(lambda: act(load(up_hbm, s.c1, 1)))

    def load_c2(act):
        pl.when(left)(lambda: act(load(up_hbm, s.c2, 2)))
        pl.when(right)(lambda: act(load(low_hbm, s.c2, 2)))

    load(d_hbm, s.diag, 0).start()
    load_c2(lambda c: c.start())
    load_c1(lambda c: c.start())
    load(b_hbm, s.rhs, 3).start()
    load(g_hbm, s.g, 4).start()

    barrier = pltpu.get_barrier_semaphore()
    for side, condition in (("partner", None), ("side", has_side), ("far", has_far)):
        guarded(condition, lambda: pl.semaphore_signal(
            barrier, inc=1, device_id=peers[side], device_id_type=pl.DeviceIdType.MESH))
    pl.semaphore_wait(barrier, 1 + jnp.where(has_side, 1, 0) + jnp.where(has_far, 1, 0))

    load_c2(lambda c: c.wait())
    send("lx", s.c2)
    send("gp", g_hbm.at[0], also=outer)

    def zero(*refs):
        for ref in refs:
            ref[...] = jnp.zeros_like(ref)

    pl.when(jnp.logical_not(has_side))(lambda: zero(s.c1, s.r_s1, s.r_st))
    pl.when(jnp.logical_not(has_far))(lambda: zero(s.r_k, s.r_z, s.r_sz))

    def cols(chunk, pieces=CHUNKS):
        return slice(chunk * (order // pieces), (chunk + 1) * (order // pieces))

    def put(pair, value, where=slice(None)):
        high = value.astype(BF16)
        pair[0, :, where] = high
        pair[1, :, where] = (value - high.astype(F32)).astype(BF16)

    def dot(left, right):
        return jnp.dot(left, right, preferred_element_type=F32)

    def multiply(left, right, where=slice(None), inside=slice(None)):
        first, second = left[0, :, inside], left[1, :, inside]
        high, low = right[0, inside, where], right[1, inside, where]
        return dot(first, high) + (dot(first, low) + dot(second, high))

    def eye(chunk):
        rows = lax.broadcasted_iota(jnp.int32, (order, width), 0)
        return (rows == lax.broadcasted_iota(jnp.int32, (order, width), 1) + chunk * width).astype(F32)

    def mean_diag():
        total = jnp.float32(0.0)
        for c in range(CHUNKS):
            total += jnp.sum(eye(c) * s.diag[:, cols(c)])
        return total / order

    def invert():
        scale = 1.0 / mean_diag()
        for c in range(CHUNKS):
            block = s.diag[:, cols(c)]
            put(s.d2, block, cols(c))
            put(s.x2, (2.0 * eye(c) - block * scale) * scale, cols(c))
        for c in range(CHUNKS):
            put(s.y2, 2.0 * eye(c) - multiply(s.d2, s.x2, cols(c)), cols(c))
        for c in range(CHUNKS):
            put(s.p2, multiply(s.x2, s.y2, cols(c)), cols(c))

    def times(left, vector):
        put(s.vec2, vector)
        return multiply(left, s.vec2)

    def coup(index):
        return s.coup.at[index]

    def prod(index):
        return s.prod.at[index]

    beyond = prod(4)
    outward = coup(jnp.where(outer, 0, 3))
    inward = coup(jnp.where(outer, 1, 2))

    load(d_hbm, s.diag, 0).wait()
    invert()
    load_c1(lambda c: c.wait())
    put(coup(0), s.c1[...])
    for c in range(CHUNKS):
        block = multiply(s.p2, coup(0), cols(c))
        s.sa1[c] = block
        send("s1", s.sa1.at[c], c, also=outer)
        send("a1", s.sa1.at[c], c)
        put(prod(0), block, cols(c))
    put(coup(1), s.c2[...])
    for c in range(CHUNKS):
        block = multiply(s.p2, coup(1), cols(c))
        s.sa2[c] = block
        send("a2", s.sa2.at[c], c)
        put(prod(1), block, cols(c))
    for c in range(CHUNKS):
        receive("a2", c)
        put(prod(3), s.r_a2[c], cols(c))

        @pl.when(inner)
        def _():
            s.sd[c] = s.diag[:, cols(c)] - multiply(coup(0), prod(3), cols(c))

        send("s1", s.sd.at[c], c, also=inner)
    load(b_hbm, s.rhs, 3).wait()
    s.sb[...] = times(s.p2, s.rhs[...])
    send("b", s.sb)
    receive("b")

    @pl.when(inner)
    def _():
        s.st[...] = s.rhs[...] - times(coup(0), s.r_b[...])

    send("gi", g_hbm.at[0])
    for c in range(CHUNKS):
        send("n", s.r_a2.at[c], c)
    send("st", s.st, also=inner)
    for c in range(FINE):
        send("lp", s.c1.at[:, cols(c, FINE)], c)

    receive("lx")

    @pl.when(inner)
    def _():
        put(coup(2), s.r_lx[...])

    second = prod(jnp.where(outer, 3, 0))
    for c in range(CHUNKS):
        put(s.in2, -multiply(inward, second, cols(c)), cols(c))
    for c in range(CHUNKS):
        receive("a1", c)
        put(prod(2), s.r_a1[c], cols(c))
    load(g_hbm, s.g, 4).wait()

    first = prod(jnp.where(outer, 2, 1))
    for c in range(CHUNKS):
        receive("s1", c)

        @pl.when(outer)
        def _():
            put(beyond, s.r_s1[c], cols(c))
            s.diag[:, cols(c)] = s.diag[:, cols(c)] - multiply(coup(0), beyond, cols(c))

        @pl.when(inner)
        def _():
            s.diag[:, cols(c)] = s.r_s1[c]

        s.diag[:, cols(c)] = s.diag[:, cols(c)] - multiply(inward, first, cols(c))

    invert()

    def scaled():
        for c in range(CHUNKS):
            put(s.k2, multiply(beyond, s.p2, cols(c)), cols(c))
        s.ssz[...] = times(beyond, s.g[...])
        send("sz", s.ssz)

    def far_piece(c):
        s.sk[c] = multiply(s.k2, outward, cols(c, FINE))
        send("k", s.sk.at[c], c)

    @pl.when(outer)
    def _():
        scaled()
        for c in range(FINE):
            far_piece(c)

    for c in range(CHUNKS):
        s.sq[c] = multiply(s.p2, s.in2, cols(c))
        send("q", s.sq.at[c], c)

    receive("gi")

    @pl.when(inner)
    def _():
        s.g[...] = s.r_gi[...]

    send("gp", s.r_gi, also=inner)
    receive("gp")
    send("st", s.sb, also=outer)
    for c in range(CHUNKS):
        receive("q", c)
        put(s.pq2, s.r_q[c], cols(c))
        s.diag[:, cols(c)] = s.diag[:, cols(c)] - multiply(s.in2, s.pq2, cols(c))
    def far_thin():
        s.pr[...] = times(s.p2, s.rhs[...] - s.acc[...])
        s.sz[...] = times(beyond, s.pr[...])
        send("z", s.sz)

    s.acc[...] = times(s.in2, s.r_gp[...])

    @pl.when(inner)
    def _():
        s.pr[...] = times(inward, s.sb[...])

    for c in range(CHUNKS):
        receive("n", c)

        @pl.when(inner)
        def _():
            put(beyond, s.r_n[c], cols(c))

    @pl.when(outer)
    def _():
        receive("st")
        s.rhs[...] = s.rhs[...] - times(coup(0), s.r_st[...]) - times(inward, s.r_b[...])
        far_thin()

    def product():
        for c in range(FINE):
            receive("k", c)
            put(s.t2, s.r_k[c], cols(c, FINE))
        for c in range(CHUNKS):
            put(s.u2, multiply(s.t2, beyond, cols(c)), cols(c))

    def piece(c):
        receive("lp", c)
        put(coup(3), s.r_lp[c], cols(c, FINE))
        far_piece(c)

    def apply(c):
        for e in range(CHUNKS):
            s.diag[:, cols(e)] = s.diag[:, cols(e)] - multiply(coup(3), s.u2, cols(e), cols(c, FINE))

    def thin():
        receive("st")
        s.rhs[...] = s.r_st[...] - s.pr[...]
        far_thin()

    @pl.when(inner)
    def _():
        scaled()
        thin()
        product()
        piece(0)
        apply(0)
        piece(1)
        apply(1)
        piece(2)
        apply(2)
        piece(3)
        apply(3)

    receive("sz")
    s.swp[...] = times(s.p2, s.rhs[...] + times(outward, s.r_sz[...]))
    send("wp", s.swp)
    receive("z")
    s.acc[...] = s.rhs[...] + times(outward, s.r_z[...])
    @pl.when(outer)
    def _():
        for c in range(FINE):
            receive("k", c)
            put(s.t2, s.r_k[c], cols(c, FINE))
            put(s.u2, multiply(outward, s.t2, cols(c, FINE)), cols(c, FINE))
            for e in range(CHUNKS):
                s.diag[:, cols(e)] = s.diag[:, cols(e)] - multiply(s.u2, beyond, cols(e), cols(c, FINE))

    receive("wp")
    s.acc[...] = s.acc[...] - times(s.in2, s.r_wp[...])

    put(s.d2, s.diag[...])
    scale = 1.0 / mean_diag()
    value = s.acc[...]
    half = (2.0 * value - times(s.d2, value) * scale) * scale
    rest = 2.0 * value - times(s.d2, half)
    result = (2.0 * rest - times(s.d2, rest) * scale) * scale

    @pl.when(outer)
    def _():
        out_ref[...] = result

    @pl.when(inner)
    def _():
        s.ssol[...] = result
        send("sol", s.ssol)
        receive("sol")
        out_ref[...] = s.r_sol[...]

    for name, _, count in MESSAGES:
        for chunk in range(max(count, 1)):
            guarded(only_if[name], lambda: copy(name, None, chunk).wait_send())


def body(diagonal, lower, upper, right_side, guess):
    across = lax.axis_size("col")
    chain = lax.axis_size("row") * across
    order, columns = right_side.shape[1:]
    types = scratch_types(order, columns)
    result = pl.pallas_call(
        functools.partial(kernel, chain, across, tuple(types)),
        out_shape=jax.ShapeDtypeStruct((order, columns), F32),
        in_specs=[pl.BlockSpec(memory_space=pl.ANY)] * 5,
        out_specs=pl.BlockSpec(memory_space=pltpu.VMEM),
        scratch_shapes=list(types.values()),
        compiler_params=pltpu.CompilerParams(
            collective_id=0, has_side_effects=True, vmem_limit_bytes=62 * 2**20),
    )(diagonal, lower, upper, right_side, guess)
    return result[None]


def solution(mesh):
    spec = P(AXES, None, None)
    return jax.shard_map(body, mesh=mesh, in_specs=(spec,) * 5, out_specs=spec, check_vma=False)
```

```python
import functools
from collections import namedtuple

import jax
import jax.numpy as jnp
from jax import lax
from jax.experimental import pallas as pl
from jax.experimental.pallas import tpu as pltpu
from jax.sharding import PartitionSpec as P

AXES = ("row", "col")
F32, BF16 = jnp.float32, jnp.bfloat16
CHUNKS = 2
FINE = 4

MESSAGES = (
    ("a1", "partner", CHUNKS), ("a2", "partner", CHUNKS), ("b", "partner", 0), ("gp", "partner", 0),
    ("q", "partner", CHUNKS), ("wp", "partner", 0),
    ("lx", "side", 1), ("s1", "side", CHUNKS), ("st", "side", 0), ("gi", "side", 0), ("lp", "side", FINE), ("n", "side", CHUNKS),
    ("sol", "side", 0),
    ("k", "far", FINE), ("z", "far", 0), ("sz", "far", 0),
)
FIRST, PEER = {}, {}
TOTAL = 0
for _name, _peer, _count in MESSAGES:
    FIRST[_name], PEER[_name] = TOTAL, _peer
    TOTAL += max(_count, 1)


def scratch_types(order, columns):
    matrix = pltpu.VMEM((order, order), F32)
    chunked = pltpu.VMEM((CHUNKS, order, order // CHUNKS), F32)
    vector = pltpu.VMEM((order, columns), F32)
    pair = pltpu.VMEM((2, order, order), BF16)
    types = dict(diag=matrix, c1=matrix, c2=matrix, rhs=vector, g=vector)
    fine = pltpu.VMEM((FINE, order, order // FINE), F32)
    types.update({name: chunked for name in ("sa1", "sa2", "sq", "sd")})
    types.update(sk=fine)
    types.update({name: vector for name in ("sb", "st", "swp", "sz", "ssz", "ssol", "pr", "acc")})
    for name, _, count in MESSAGES:
        types["r_" + name] = {0: vector, 1: matrix, CHUNKS: chunked, FINE: fine}[count]
    types.update({name: pair for name in ("d2", "x2", "y2", "p2", "in2", "k2", "t2", "u2", "pq2")})
    types.update(coup=pltpu.VMEM((4, 2, order, order), BF16), prod=pltpu.VMEM((5, 2, order, order), BF16))
    types.update(vec2=pltpu.VMEM((2, order, columns), BF16), wide2=pltpu.VMEM((2, order, 2 * columns), BF16))
    types.update(load_sem=pltpu.SemaphoreType.DMA((5,)))
    types.update(send_sem=pltpu.SemaphoreType.DMA((TOTAL,)), recv_sem=pltpu.SemaphoreType.DMA((TOTAL,)))
    return types


def kernel(chain, across, names, d_hbm, low_hbm, up_hbm, b_hbm, g_hbm, out_ref, *scratch):
    s = namedtuple("Scratch", names)(*scratch)
    order = s.diag.shape[0]
    width = order // CHUNKS
    place = lax.axis_index("row") * across + lax.axis_index("col")
    role = lax.rem(place, 4)
    outer = (role == 0) | (role == 3)
    inner = (role == 1) | (role == 2)
    left = role < 2
    right = role >= 2
    away = 2 * lax.rem(place, 2) - 1
    has_side = (place + away >= 0) & (place + away < chain)
    has_far = (place + 3 * away >= 0) & (place + 3 * away < chain)

    def device(offset):
        index = lax.rem(place + offset + chain, chain)
        return (index // across, lax.rem(index, across))

    peers = {"partner": device(-away), "side": device(away), "far": device(3 * away)}
    exists = {"partner": None, "side": has_side, "far": has_far}
    only_if = {name: exists[peer] for name, peer in PEER.items()}
    only_if.update({name: inner for name in ("lx", "gi", "n", "lp", "sol")})

    def guarded(condition, action):
        if condition is None:
            action()
        else:
            pl.when(condition)(action)

    def copy(name, src, chunk):
        dst = getattr(s, "r_" + name)
        index = FIRST[name] + chunk
        if dst.ndim == 3:
            dst = dst.at[chunk]
        return pltpu.make_async_remote_copy(
            src_ref=src if src is not None else dst,
            dst_ref=dst,
            send_sem=s.send_sem.at[index],
            recv_sem=s.recv_sem.at[index],
            device_id=peers[PEER[name]],
            device_id_type=pl.DeviceIdType.MESH,
        )

    def send(name, src, chunk=0, also=None):
        condition = only_if[name]
        if also is not None:
            condition = also if condition is None else condition & also
        guarded(condition, lambda: copy(name, src, chunk).start())

    def receive(name, chunk=0):
        guarded(only_if[name], lambda: copy(name, None, chunk).wait_recv())

    def load(src, dst, index):
        return pltpu.make_async_copy(src.at[0], dst, s.load_sem.at[index])

    def load_c1(act):
        pl.when(has_side & left)(lambda: act(load(low_hbm, s.c1, 1)))
        pl.when(has_side & right)(lambda: act(load(up_hbm, s.c1, 1)))

    def load_c2(act):
        pl.when(left)(lambda: act(load(up_hbm, s.c2, 2)))
        pl.when(right)(lambda: act(load(low_hbm, s.c2, 2)))

    load(d_hbm, s.diag, 0).start()
    load_c2(lambda c: c.start())
    load_c1(lambda c: c.start())
    load(b_hbm, s.rhs, 3).start()
    load(g_hbm, s.g, 4).start()

    barrier = pltpu.get_barrier_semaphore()
    for side, condition in (("partner", None), ("side", has_side), ("far", has_far)):
        guarded(condition, lambda: pl.semaphore_signal(
            barrier, inc=1, device_id=peers[side], device_id_type=pl.DeviceIdType.MESH))
    pl.semaphore_wait(barrier, 1 + jnp.where(has_side, 1, 0) + jnp.where(has_far, 1, 0))

    load_c2(lambda c: c.wait())
    send("lx", s.c2)
    send("gp", g_hbm.at[0], also=outer)

    def zero(*refs):
        for ref in refs:
            ref[...] = jnp.zeros_like(ref)

    pl.when(jnp.logical_not(has_side))(lambda: zero(s.c1, s.r_s1, s.r_st))
    pl.when(jnp.logical_not(has_far))(lambda: zero(s.r_k, s.r_z, s.r_sz))

    def cols(chunk, pieces=CHUNKS):
        return slice(chunk * (order // pieces), (chunk + 1) * (order // pieces))

    def put(pair, value, where=slice(None)):
        high = value.astype(BF16)
        pair[0, :, where] = high
        pair[1, :, where] = (value - high.astype(F32)).astype(BF16)

    def dot(left, right):
        return jnp.dot(left, right, preferred_element_type=F32)

    def multiply(left, right, where=slice(None), inside=slice(None)):
        first, second = left[0, :, inside], left[1, :, inside]
        high, low = right[0, inside, where], right[1, inside, where]
        return dot(first, high) + (dot(first, low) + dot(second, high))

    def eye(chunk):
        rows = lax.broadcasted_iota(jnp.int32, (order, width), 0)
        return (rows == lax.broadcasted_iota(jnp.int32, (order, width), 1) + chunk * width).astype(F32)

    def mean_diag():
        total = jnp.float32(0.0)
        for c in range(CHUNKS):
            total += jnp.sum(eye(c) * s.diag[:, cols(c)])
        return total / order

    def invert():
        scale = 1.0 / mean_diag()
        for c in range(CHUNKS):
            block = s.diag[:, cols(c)]
            put(s.d2, block, cols(c))
            put(s.x2, (2.0 * eye(c) - block * scale) * scale, cols(c))
        for c in range(CHUNKS):
            put(s.y2, 2.0 * eye(c) - multiply(s.d2, s.x2, cols(c)), cols(c))
        for c in range(CHUNKS):
            put(s.p2, multiply(s.x2, s.y2, cols(c)), cols(c))

    def times(left, vector):
        put(s.vec2, vector)
        return multiply(left, s.vec2)

    def coup(index):
        return s.coup.at[index]

    def prod(index):
        return s.prod.at[index]

    beyond = prod(4)
    outward = coup(jnp.where(outer, 0, 3))
    inward = coup(jnp.where(outer, 1, 2))

    load(d_hbm, s.diag, 0).wait()
    invert()
    load_c1(lambda c: c.wait())
    put(coup(0), s.c1[...])
    for c in range(CHUNKS):
        block = multiply(s.p2, coup(0), cols(c))
        s.sa1[c] = block
        send("s1", s.sa1.at[c], c, also=outer)
        send("a1", s.sa1.at[c], c)
        put(prod(0), block, cols(c))
    put(coup(1), s.c2[...])
    for c in range(CHUNKS):
        block = multiply(s.p2, coup(1), cols(c))
        s.sa2[c] = block
        send("a2", s.sa2.at[c], c)
        put(prod(1), block, cols(c))
    for c in range(CHUNKS):
        receive("a2", c)
        put(prod(3), s.r_a2[c], cols(c))

        @pl.when(inner)
        def _():
            s.sd[c] = s.diag[:, cols(c)] - multiply(coup(0), prod(3), cols(c))

        send("s1", s.sd.at[c], c, also=inner)
    load(b_hbm, s.rhs, 3).wait()
    s.sb[...] = times(s.p2, s.rhs[...])
    send("b", s.sb)
    receive("b")

    @pl.when(inner)
    def _():
        s.st[...] = s.rhs[...] - times(coup(0), s.r_b[...])

    send("gi", g_hbm.at[0])
    for c in range(CHUNKS):
        send("n", s.r_a2.at[c], c)
    send("st", s.st, also=inner)
    for c in range(FINE):
        send("lp", s.c1.at[:, cols(c, FINE)], c)

    receive("lx")

    @pl.when(inner)
    def _():
        put(coup(2), s.r_lx[...])

    second = prod(jnp.where(outer, 3, 0))
    for c in range(CHUNKS):
        put(s.in2, -multiply(inward, second, cols(c)), cols(c))
    for c in range(CHUNKS):
        receive("a1", c)
        put(prod(2), s.r_a1[c], cols(c))
    load(g_hbm, s.g, 4).wait()

    first = prod(jnp.where(outer, 2, 1))
    for c in range(CHUNKS):
        receive("s1", c)

        @pl.when(outer)
        def _():
            put(beyond, s.r_s1[c], cols(c))
            s.diag[:, cols(c)] = s.diag[:, cols(c)] - multiply(coup(0), beyond, cols(c))

        @pl.when(inner)
        def _():
            s.diag[:, cols(c)] = s.r_s1[c]

        s.diag[:, cols(c)] = s.diag[:, cols(c)] - multiply(inward, first, cols(c))

    invert()

    def scaled():
        for c in range(CHUNKS):
            put(s.k2, multiply(beyond, s.p2, cols(c)), cols(c))
        s.ssz[...] = times(beyond, s.g[...])
        send("sz", s.ssz)

    def far_piece(c):
        s.sk[c] = multiply(s.k2, outward, cols(c, FINE))
        send("k", s.sk.at[c], c)

    @pl.when(outer)
    def _():
        scaled()
        for c in range(FINE):
            far_piece(c)

    for c in range(CHUNKS):
        s.sq[c] = multiply(s.p2, s.in2, cols(c))
        send("q", s.sq.at[c], c)

    receive("gi")

    @pl.when(inner)
    def _():
        s.g[...] = s.r_gi[...]

    send("gp", s.r_gi, also=inner)
    receive("gp")
    send("st", s.sb, also=outer)
    for c in range(CHUNKS):
        receive("q", c)
        put(s.pq2, s.r_q[c], cols(c))
        s.diag[:, cols(c)] = s.diag[:, cols(c)] - multiply(s.in2, s.pq2, cols(c))
    def far_thin():
        s.pr[...] = times(s.p2, s.rhs[...] - s.acc[...])
        s.sz[...] = times(beyond, s.pr[...])
        send("z", s.sz)

    s.acc[...] = times(s.in2, s.r_gp[...])

    @pl.when(inner)
    def _():
        s.pr[...] = times(inward, s.sb[...])

    for c in range(CHUNKS):
        receive("n", c)

        @pl.when(inner)
        def _():
            put(beyond, s.r_n[c], cols(c))

    @pl.when(outer)
    def _():
        receive("st")
        s.rhs[...] = s.rhs[...] - times(coup(0), s.r_st[...]) - times(inward, s.r_b[...])
        far_thin()

    def product():
        for c in range(FINE):
            receive("k", c)
            put(s.t2, s.r_k[c], cols(c, FINE))
        for c in range(CHUNKS):
            put(s.u2, multiply(s.t2, beyond, cols(c)), cols(c))

    def piece(c):
        receive("lp", c)
        put(coup(3), s.r_lp[c], cols(c, FINE))
        far_piece(c)

    def apply(c):
        for e in range(CHUNKS):
            s.diag[:, cols(e)] = s.diag[:, cols(e)] - multiply(coup(3), s.u2, cols(e), cols(c, FINE))

    def thin():
        receive("st")
        s.rhs[...] = s.r_st[...] - s.pr[...]
        far_thin()

    @pl.when(inner)
    def _():
        scaled()
        thin()
        product()
        piece(0)
        apply(0)
        piece(1)
        apply(1)
        piece(2)
        apply(2)
        piece(3)
        apply(3)

    columns = s.rhs.shape[1]
    receive("sz")
    put(s.wide2, s.r_sz[...], slice(0, columns))
    receive("z")
    put(s.wide2, s.r_z[...], slice(columns, 2 * columns))
    both = multiply(outward, s.wide2)
    s.acc[...] = s.rhs[...] + both[:, columns:]
    s.swp[...] = times(s.p2, s.rhs[...] + both[:, :columns])
    send("wp", s.swp)
    @pl.when(outer)
    def _():
        for c in range(FINE):
            receive("k", c)
            put(s.t2, s.r_k[c], cols(c, FINE))
            put(s.u2, multiply(outward, s.t2, cols(c, FINE)), cols(c, FINE))
            for e in range(CHUNKS):
                s.diag[:, cols(e)] = s.diag[:, cols(e)] - multiply(s.u2, beyond, cols(e), cols(c, FINE))

    receive("wp")
    s.acc[...] = s.acc[...] - times(s.in2, s.r_wp[...])

    put(s.d2, s.diag[...])
    scale = 1.0 / mean_diag()
    value = s.acc[...]
    half = (2.0 * value - times(s.d2, value) * scale) * scale
    rest = 2.0 * value - times(s.d2, half)
    result = (2.0 * rest - times(s.d2, rest) * scale) * scale

    @pl.when(outer)
    def _():
        out_ref[...] = result

    @pl.when(inner)
    def _():
        s.ssol[...] = result
        send("sol", s.ssol)
        receive("sol")
        out_ref[...] = s.r_sol[...]

    for name, _, count in MESSAGES:
        for chunk in range(max(count, 1)):
            guarded(only_if[name], lambda: copy(name, None, chunk).wait_send())


def body(diagonal, lower, upper, right_side, guess):
    across = lax.axis_size("col")
    chain = lax.axis_size("row") * across
    order, columns = right_side.shape[1:]
    types = scratch_types(order, columns)
    result = pl.pallas_call(
        functools.partial(kernel, chain, across, tuple(types)),
        out_shape=jax.ShapeDtypeStruct((order, columns), F32),
        in_specs=[pl.BlockSpec(memory_space=pl.ANY)] * 5,
        out_specs=pl.BlockSpec(memory_space=pltpu.VMEM),
        scratch_shapes=list(types.values()),
        compiler_params=pltpu.CompilerParams(
            collective_id=0, has_side_effects=True, vmem_limit_bytes=62 * 2**20),
    )(diagonal, lower, upper, right_side, guess)
    return result[None]


def solution(mesh):
    spec = P(AXES, None, None)
    return jax.shard_map(body, mesh=mesh, in_specs=(spec,) * 5, out_specs=spec, check_vma=False)
```
